32 devices in a mesh: dp: 2 (over y), row: 4 (over z), col: 4 (over x, core).
Axes of the slice: x: 2, y: 2, z: 4, core: 2. Of those that a mesh axis runs over, the one named last changes fastest.
Arguments:
- residual_in: float32 [2, 8192, 1024], P(None, ('dp', 'row'), 'col'), may hold values from -57 to 57
- encoder_out: float32 [2, 8000, 1024], P(None, ('dp', 'row'), 'col'), may hold values from -6 to 6
- prefix_len: int32 [2, 8], P(None, ('dp', 'row')), may hold values from 102 to 512
- bucket_table: int32 [2047], replicated, may hold values from 0 to 31
- cotangent: float32 [2, 8192, 1024], P(None, ('dp', 'row'), 'col'), may hold values from -6 to 6
- norm_self: float32 [1024], P('col'), may hold values from 0.5 to 1.5
- norm_cross: float32 [1024], P('col'), may hold values from 0.5 to 1.5
- norm_ffn: float32 [1024], P('col'), may hold values from 0.5 to 1.5
- self_query: float32 [1024, 1024], P('row', 'col'), may hold values from -0.0625 to 0.0625
- self_key: float32 [1024, 1024], P('row', 'col'), may hold values from -0.1875 to 0.1875
- self_value: float32 [1024, 1024], P('row', 'col'), may hold values from -0.1875 to 0.1875
- self_out: float32 [1024, 1024], P('col', 'row'), may hold values from -0.375 to 0.375
- cross_query: float32 [1024, 1024], P('row', 'col'), may hold values from -0.046875 to 0.046875
- cross_key: float32 [1024, 1024], P('row', 'col'), may hold values from -0.1875 to 0.1875
- cross_value: float32 [1024, 1024], P('row', 'col'), may hold values from -0.1875 to 0.1875
- cross_out: float32 [1024, 1024], P('col', 'row'), may hold values from -0.375 to 0.375
- ffn_in: float32 [1024, 4096], P('row', 'col'), may hold values from -0.1875 to 0.1875
- ffn_out: float32 [4096, 1024], P('col', 'row'), may hold values from -0.125 to 0.125
- rel_bias: float32 [32, 16], P('row', 'col'), may hold values from -4 to 4
Outputs:
- layer_out: float32 [2, 8192, 1024], P(None, ('dp', 'row'), 'col')
- grad_residual: float32 [2, 8192, 1024], P(None, ('dp', 'row'), 'col')
- grad_encoder: float32 [2, 8000, 1024], P(None, ('dp', 'row'), 'col')
- grad_norm_self: float32 [1024], P('col')
- grad_norm_cross: float32 [1024], P('col')
- grad_norm_ffn: float32 [1024], P('col')
- grad_self_query: float32 [1024, 1024], P(('dp', 'row'), 'col')
- grad_self_key: float32 [1024, 1024], P(('dp', 'row'), 'col')
- grad_self_value: float32 [1024, 1024], P(('dp', 'row'), 'col')
- grad_self_out: float32 [1024, 1024], P('col', ('dp', 'row'))
- grad_cross_query: float32 [1024, 1024], P(('dp', 'row'), 'col')
- grad_cross_key: float32 [1024, 1024], P(('dp', 'row'), 'col')
- grad_cross_value: float32 [1024, 1024], P(('dp', 'row'), 'col')
- grad_cross_out: float32 [1024, 1024], P('col', ('dp', 'row'))
- grad_ffn_in: float32 [1024, 4096], P(('dp', 'row'), 'col')
- grad_ffn_out: float32 [4096, 1024], P('col', ('dp', 'row'))
- grad_rel_bias: float32 [32, 16], P(('dp', 'row'), 'col')
The draws below stay inside these ranges and needn't reach their ends.
Inputs may be any that keep to these rules, and one draw needn't show every extreme that they name: The first prefix_len[m, s] tokens of a sequence attend to each other both ways.
All inputs are finite; a program needn't handle non-finite values.
Results may differ from the reference program's by a relative error of at most 0.029.
Values may be sent and summed in bfloat16 or wider, within the bound.
No kernel may reach another device: no remote copies, remote signals or barrier semaphores. Data moves between devices by JAX's collectives and lax.ppermute only.
A program may use at most 832 MiB of HBM per device.

```python
import jax
import jax.numpy as jnp
from jax import lax

D = 1024
HEADS = 16
HEAD_DIM = 64
FF = 4096
BUCKETS = 32
LEN = 1024
MICRO = 2
INNER = 1024
MEM = 1000
SEQS_MB = 8
TOK_MB = 8192
MEM_MB = 8000


def draw_residual_in(key, part):
    noise_key = jax.random.fold_in(key, 11)
    place_key = jax.random.fold_in(key, 12)
    size_key = jax.random.fold_in(key, 13)
    sign_key = jax.random.fold_in(key, 14)
    row_key = jax.random.fold_in(key, 15)
    noise = jax.random.truncated_normal(noise_key, -6.0, 6.0, (MICRO, TOK_MB, D), jnp.float32)
    place = jax.random.randint(place_key, (), 0, D)
    sign_int = jax.random.randint(sign_key, (), 0, 2)
    sign_val = 2.0 * sign_int.astype(jnp.float32) - 1.0
    magnitude = jax.random.uniform(size_key, (), jnp.float32, 0.875, 1.125) * (D / 32.0)
    row_factor = jax.random.uniform(row_key, (MICRO, TOK_MB, 1), jnp.float32, 0.75, 1.25)
    column = (jnp.arange(D, dtype=jnp.int32) == place).astype(jnp.float32)
    return noise + sign_val * magnitude * row_factor * column


def place_ends(entries, rng, least, top_value):
    index_at = [jax.random.randint(jax.random.fold_in(rng, axis), (), 0, length) for axis, length in enumerate(entries.shape)]
    main_axis = entries.shape.index(max(entries.shape))
    next_to = index_at[:main_axis] + [(index_at[main_axis] + 1) % entries.shape[main_axis]] + index_at[main_axis + 1:]
    return entries.at[tuple(index_at)].set(least).at[tuple(next_to)].set(top_value)


def level_of(key, shape, cuts, low, high):
    factor_of, own = 1.0, jax.random.fold_in(key, 6)
    for position, blocks in cuts:
        steps = jnp.exp(jax.random.uniform(jax.random.fold_in(own, position), (blocks,), jnp.float32, low / len(cuts), high / len(cuts)))
        factor_of = factor_of * jnp.repeat(steps, shape[position] // blocks).reshape([-1 if axis == position else 1 for axis in range(len(shape))])
    return factor_of


def bell_draw(stream_key, dims, deviation, limit, shards=(), kind=jnp.bfloat16):
    values = deviation * jax.random.normal(stream_key, dims, jnp.float32)
    if shards:
        values = values * level_of(stream_key, dims, shards, -0.22, 0.18)
    return jnp.clip(values, -limit, limit).astype(kind)


def setup_inputs(seed: int = 0) -> dict:
    splits = jax.random.split(jax.random.key(seed), 20)
    residual_in = draw_residual_in(jax.random.fold_in(splits[19], 71), 0)
    encoder_out = bell_draw(splits[1], (MICRO, MEM_MB, D), 1.0, 6.0, ((1, 8), (2, 4)), jnp.float32)
    prefix_len = place_ends(jax.random.randint(splits[2], (MICRO, SEQS_MB), LEN // 10, LEN // 2 + 1), jax.random.fold_in(splits[2], 1), LEN // 10, (LEN // 2 + 1) - 1).astype(jnp.int32)
    bucket_table = place_ends(jax.random.randint(splits[3], (2 * LEN - 1,), 0, BUCKETS), jax.random.fold_in(splits[3], 1), 0, BUCKETS - 1).astype(jnp.int32)
    cotangent = bell_draw(splits[4], (MICRO, TOK_MB, D), 1.0, 6.0, ((1, 8), (2, 4)), jnp.float32)
    norm_self = jnp.clip(1.0 + 0.1 * jax.random.normal(splits[5], (D,), jnp.float32), 0.5, 1.5)
    norm_cross = jnp.clip(1.0 + 0.1 * jax.random.normal(splits[6], (D,), jnp.float32), 0.5, 1.5)
    norm_ffn = jnp.clip(1.0 + 0.1 * jax.random.normal(splits[7], (D,), jnp.float32), 0.5, 1.5)
    self_query = bell_draw(splits[8], (D, INNER), (D * HEAD_DIM // 8) ** -0.5, 0.0625, ((0, 4), (1, 4)), jnp.float32)
    self_key = bell_draw(splits[9], (D, INNER), D ** -0.5, 0.1875, ((0, 4), (1, 4)), jnp.float32)
    self_value = bell_draw(splits[10], (D, INNER), D ** -0.5, 0.1875, ((0, 4), (1, 4)), jnp.float32)
    self_out = bell_draw(splits[11], (INNER, D), (INNER // 4) ** -0.5, 0.375, ((0, 4), (1, 4)), jnp.float32)
    cross_query = bell_draw(splits[12], (D, INNER), (D * HEAD_DIM // 4) ** -0.5, 0.046875, ((0, 4), (1, 4)), jnp.float32)
    cross_key = bell_draw(splits[13], (D, INNER), D ** -0.5, 0.1875, ((0, 4), (1, 4)), jnp.float32)
    cross_value = bell_draw(splits[14], (D, INNER), D ** -0.5, 0.1875, ((0, 4), (1, 4)), jnp.float32)
    cross_out = bell_draw(splits[15], (INNER, D), (INNER // 4) ** -0.5, 0.375, ((0, 4), (1, 4)), jnp.float32)
    ffn_in = bell_draw(splits[16], (D, FF), D ** -0.5, 0.1875, ((0, 4), (1, 4)), jnp.float32)
    ffn_out = bell_draw(splits[17], (FF, D), (FF // 2) ** -0.5, 0.125, ((0, 4), (1, 4)), jnp.float32)
    rel_bias = bell_draw(splits[18], (BUCKETS, HEADS), 1.0, 4.0, ((0, 4), (1, 4)), jnp.float32)
    return dict(residual_in=residual_in, encoder_out=encoder_out, prefix_len=prefix_len, bucket_table=bucket_table, cotangent=cotangent, norm_self=norm_self, norm_cross=norm_cross, norm_ffn=norm_ffn, self_query=self_query, self_key=self_key, self_value=self_value, self_out=self_out, cross_query=cross_query, cross_key=cross_key, cross_value=cross_value, cross_out=cross_out, ffn_in=ffn_in, ffn_out=ffn_out, rel_bias=rel_bias)


@jax.custom_vjp
def low(v):
    return lax.optimization_barrier(v.astype(jnp.bfloat16)).astype(jnp.float32)

@jax.custom_vjp
def low_back(v):
    return v

def low_keep(v):
    return (low(v), None)

def low_pass(kept, grad):
    return (grad,)

def back_keep(v):
    return (v, None)

def back_low(kept, grad):
    return (low(grad),)
low.defvjp(low_keep, low_pass)
low_back.defvjp(back_keep, back_low)

def rms_norm(values, gain_vec):
    return values * lax.rsqrt(lax.optimization_barrier(jnp.mean(values * values, axis=-1, keepdims=True)) + 1e-06) * gain_vec

def matmul(left, right):
    return jnp.dot(left, right, precision=lax.Precision.HIGHEST, preferred_element_type=jnp.float32)

def attend(queries, key_rows, value_rows, pos_bias, allowed):
    length = queries.shape[0]
    key_count = key_rows.shape[0]
    query_heads = queries.reshape(length, HEADS, HEAD_DIM)
    key_heads = key_rows.reshape(key_count, HEADS, HEAD_DIM)
    value_heads = value_rows.reshape(key_count, HEADS, HEAD_DIM)
    scores = jnp.einsum('qhe,khe->hqk', query_heads, key_heads, precision=lax.Precision.HIGHEST) + pos_bias
    scores = jnp.where(allowed[None], low_back(scores), -1000000000.0)
    attn_probs = low(jax.nn.softmax(scores, axis=-1))
    mixed = jnp.einsum('hqk,khe->qhe', attn_probs, value_heads, precision=lax.Precision.HIGHEST)
    return low(low_back(mixed.reshape(length, HEADS * HEAD_DIM)))

def decoder_layer(params, resid_in, memory_in, allowed, cross_allowed, bucket_ids):
    rounded = [low(item) for item in params[3:]]
    attend_ckpt = jax.checkpoint(attend)
    pos_bias = jnp.transpose(rounded[10][bucket_ids], (2, 0, 1))
    normed_one = low(rms_norm(resid_in, params[0]))
    queries = low(low_back(matmul(normed_one, rounded[0])))
    key_rows = low(low_back(matmul(normed_one, rounded[1])))
    value_rows = low(low_back(matmul(normed_one, rounded[2])))
    self_mix = attend_ckpt(queries, key_rows, value_rows, pos_bias, allowed)
    resid_one = resid_in + low_back(matmul(self_mix, rounded[3]))
    normed_two = low(rms_norm(resid_one, params[1]))
    memory_low = low(memory_in)
    cross_queries = low(low_back(matmul(normed_two, rounded[4])))
    cross_keys = low(low_back(matmul(memory_low, rounded[5])))
    cross_values = low(low_back(matmul(memory_low, rounded[6])))
    no_bias = jnp.zeros((), jnp.float32)
    cross_mix = attend_ckpt(cross_queries, cross_keys, cross_values, no_bias, cross_allowed)
    resid_two = resid_one + low_back(matmul(cross_mix, rounded[7]))
    normed_three = low(rms_norm(resid_two, params[2]))
    ffn_pre = low_back(matmul(normed_three, rounded[8]))
    ffn_act = low(jax.nn.gelu(ffn_pre, approximate=True))
    return resid_two + low_back(matmul(ffn_act, rounded[9]))

def reference(residual_in, encoder_out, prefix_len, bucket_table, cotangent, norm_self, norm_cross, norm_ffn, self_query, self_key, self_value, self_out, cross_query, cross_key, cross_value, cross_out, ffn_in, ffn_out, rel_bias):
    seq_total = residual_in.shape[0] * (residual_in.shape[1] // LEN)
    inputs = residual_in.reshape(seq_total, LEN, D)
    memories = encoder_out.reshape(seq_total, MEM, D)
    prefixes = prefix_len.reshape(seq_total)
    cotangents = cotangent.reshape(seq_total, LEN, D)
    params = (norm_self, norm_cross, norm_ffn, self_query, self_key, self_value, self_out, cross_query, cross_key, cross_value, cross_out, ffn_in, ffn_out, rel_bias)
    places = jnp.arange(LEN, dtype=jnp.int32)
    bucket_ids = bucket_table[(places[None, :] - places[:, None] + LEN - 1).astype(jnp.int32)]
    cross_allowed = jnp.ones((LEN, MEM), dtype=bool)

    def per_sequence(running, pieces):
        resid_in, memory_in, cut_len, cot_in = pieces
        allowed = (places[None, :] <= places[:, None]) | (places[None, :] < cut_len)

        def forward(weights, resid_arg, memory_arg):
            return decoder_layer(weights, resid_arg, memory_arg, allowed, cross_allowed, bucket_ids)
        layer_rows, pull_back = jax.vjp(forward, params, resid_in, memory_in)
        grad_params, grad_resid, grad_mem = pull_back(cot_in)
        running = jax.tree.map(lambda total_val, fresh: total_val + fresh, running, grad_params)
        return (running, (layer_rows, grad_resid, grad_mem))
    start_sums = jax.tree.map(jnp.zeros_like, params)
    grad_sums, (layer_outs, grad_inputs, grad_memories) = lax.scan(per_sequence, start_sums, (inputs, memories, prefixes, cotangents))
    return (layer_outs.reshape(residual_in.shape), grad_inputs.reshape(residual_in.shape), grad_memories.reshape(encoder_out.shape), grad_sums[0], grad_sums[1], grad_sums[2], grad_sums[3], grad_sums[4], grad_sums[5], grad_sums[6], grad_sums[7], grad_sums[8], grad_sums[9], grad_sums[10], grad_sums[11], grad_sums[12], grad_sums[13])
```

```python
import functools

import jax
import jax.numpy as jnp
from jax import lax
from jax.experimental import pallas as pl
from jax.experimental.pallas import tpu as pltpu
from jax.sharding import PartitionSpec as P

NEG_FILL = -1000000000.0
BLOCK = 256
PAIR = 128


def project(left, right):
    return jnp.dot(left, right, preferred_element_type=jnp.float32)


def project_back(left, right):
    return lax.dot_general(
        left, right, (((1,), (1,)), ((), ())), preferred_element_type=jnp.float32
    )


def project_left(left, right):
    return lax.dot_general(
        left, right, (((0,), (0,)), ((), ())), preferred_element_type=jnp.float32
    )


def smooth_act(values):
    return jax.nn.gelu(values, approximate=True)


def dot_nt(left, right):
    return lax.dot_general(left, right, (((1,), (1,)), ((), ())), preferred_element_type=jnp.float32)


def dot_nn(left, right):
    return lax.dot_general(left, right, (((1,), (0,)), ((), ())), preferred_element_type=jnp.float32)


def head_mask(head, head_size):
    lane = lax.broadcasted_iota(jnp.int32, (1, PAIR), 1)
    low = head * head_size
    return ((lane >= low) & (lane < low + head_size)).astype(jnp.float32)


def key_blocks(q_block, key_count, self_mode, prefix_blocks):
    total = key_count // BLOCK
    return min(total, max(q_block + 1, prefix_blocks)) if self_mode else total


def forward_kernel(self_mode, q_count, key_count, key_valid, head_size, prefix_blocks, *refs):
    if self_mode:
        cut_ref, vec_ref, q_ref, k_ref, v_ref, o_ref, rest_ref, lse_ref, band = refs
    else:
        q_ref, k_ref, v_ref, o_ref, rest_ref, lse_ref = refs
    head = pl.program_id(1)
    mask = head_mask(head, head_size)
    mask_low = mask.astype(jnp.bfloat16)
    if self_mode:
        wide = jnp.broadcast_to(vec_ref[0], (BLOCK, band.shape[1]))
        band[...] = pltpu.roll(wide, 0, 1, stride=1, stride_axis=0)
        cut = cut_ref[0]
    base = q_count - BLOCK
    col = lax.broadcasted_iota(jnp.int32, (BLOCK, BLOCK), 1)
    row = lax.broadcasted_iota(jnp.int32, (BLOCK, BLOCK), 0)
    for qb in range(q_count // BLOCK):
        q_rows = pl.ds(qb * BLOCK, BLOCK)
        query = q_ref[q_rows, :] * mask_low
        parts = []
        for kb in range(key_blocks(qb, key_count, self_mode, prefix_blocks)):
            s = dot_nt(query, k_ref[pl.ds(kb * BLOCK, BLOCK), :])
            if self_mode:
                s = s + band[:, pl.ds((kb - qb) * BLOCK + base, BLOCK)]
                if kb >= qb:
                    limit = jnp.maximum(row + qb * BLOCK, cut - 1)
                    s = jnp.where(col + kb * BLOCK <= limit, s, NEG_FILL)
            elif (kb + 1) * BLOCK > key_valid:
                s = jnp.where(col + kb * BLOCK < key_valid, s, NEG_FILL)
            parts.append(s)
        top = functools.reduce(jnp.maximum, [jnp.max(s, axis=1, keepdims=True) for s in parts])
        total = jnp.zeros((BLOCK, 1), jnp.float32)
        mixed = jnp.zeros((BLOCK, PAIR), jnp.float32)
        for kb, s in enumerate(parts):
            e = jnp.exp(s - top)
            total = total + jnp.sum(e, axis=1, keepdims=True)
            mixed = mixed + dot_nn(e.astype(jnp.bfloat16), v_ref[pl.ds(kb * BLOCK, BLOCK), :])
        mixed = mixed * (mask / total)
        mixed_low = mixed.astype(jnp.bfloat16)
        rest = (mixed - mixed_low.astype(jnp.float32)).astype(jnp.bfloat16)

        @pl.when(head == 0)
        def _():
            o_ref[q_rows, :] = mixed_low
            rest_ref[q_rows, :] = rest

        @pl.when(head > 0)
        def _():
            o_ref[q_rows, :] += mixed_low
            rest_ref[q_rows, :] += rest

        log_total = jnp.broadcast_to(top + jnp.log(total), (BLOCK, PAIR))
        lse_ref[0, :, q_rows] = log_total.T[:1]


def backward_kernel(self_mode, q_count, key_count, key_valid, head_size, prefix_blocks, *refs):
    if self_mode:
        cut_ref, vec_ref, q_ref, k_ref, v_ref, o_ref, rest_ref, do_ref, lse_ref = refs[:9]
        dq_ref, dk_ref, dv_ref, diag_ref, kt, dqt, dk_acc, dv_acc, band, acc = refs[9:]
    else:
        q_ref, k_ref, v_ref, o_ref, rest_ref, do_ref, lse_ref = refs[:7]
        dq_ref, dk_ref, dv_ref, kt, dqt, dk_acc, dv_acc = refs[7:]
    head = pl.program_id(1)
    mask = head_mask(head, head_size)
    mask_low = mask.astype(jnp.bfloat16)
    base = q_count - BLOCK

    @pl.when(head == 0)
    def _():
        kt[...] = k_ref[...].T
        dk_acc[...] = jnp.zeros_like(dk_acc)
        dv_acc[...] = jnp.zeros_like(dv_acc)

    if self_mode:
        wide = jnp.broadcast_to(vec_ref[0], (BLOCK, band.shape[1]))
        band[...] = pltpu.roll(wide, 0, 1, stride=1, stride_axis=0)
        acc[...] = jnp.zeros_like(acc)
        cut = cut_ref[0]
    col = lax.broadcasted_iota(jnp.int32, (BLOCK, BLOCK), 1)
    row = lax.broadcasted_iota(jnp.int32, (BLOCK, BLOCK), 0)
    head_rows = pl.ds(pl.multiple_of(head * head_size, head_size), head_size)
    key_t = kt[head_rows, :]
    for qb in range(q_count // BLOCK):
        q_rows = pl.ds(qb * BLOCK, BLOCK)
        query = q_ref[q_rows, :] * mask_low
        grad = do_ref[q_rows, :] * mask_low
        mixed = o_ref[q_rows, :].astype(jnp.float32) + rest_ref[q_rows, :].astype(jnp.float32)
        product = grad.astype(jnp.float32) * mixed
        delta = jnp.sum(product.T, axis=0, keepdims=True)
        log_total = lse_ref[0, :, q_rows]
        dqt_sum = jnp.zeros((head_size, BLOCK), jnp.float32)
        for kb in range(key_blocks(qb, key_count, self_mode, prefix_blocks)):
            k_rows = pl.ds(kb * BLOCK, BLOCK)
            s = dot_nt(k_ref[k_rows, :], query)
            dp = dot_nt(v_ref[k_rows, :], grad)
            if self_mode:
                span = pl.ds((qb - kb) * BLOCK + base, BLOCK)
                s = s + band[:, span]
                if kb >= qb:
                    limit = jnp.maximum(col + qb * BLOCK, cut - 1)
                    s = jnp.where(row + kb * BLOCK <= limit, s, NEG_FILL)
            elif (kb + 1) * BLOCK > key_valid:
                s = jnp.where(row + kb * BLOCK < key_valid, s, NEG_FILL)
            p = jnp.exp(s - log_total)
            ds = p * (dp - delta)
            ds_low = ds.astype(jnp.bfloat16)
            if self_mode:
                acc[:, span] += ds
            dv_acc[k_rows, :] += dot_nn(p.astype(jnp.bfloat16), grad)
            dk_acc[k_rows, :] += dot_nn(ds_low, query)
            dqt_sum = dqt_sum + dot_nn(key_t[:, kb * BLOCK : (kb + 1) * BLOCK], ds_low)
        dqt[head_rows, q_rows] = dqt_sum
    if self_mode:
        size = BLOCK
        fold = acc[...]
        lanes = fold.shape[1]
        while size > 8:
            size //= 2
            fold = fold[:size] + pltpu.roll(fold[size:], lanes - size, 1)
        diag_ref[0] = fold

    @pl.when(head == pl.num_programs(1) - 1)
    def _():
        dq_ref[...] = dqt[...].T.astype(jnp.bfloat16)
        dk_ref[...] = dk_acc[...].astype(jnp.bfloat16)
        dv_ref[...] = dv_acc[...].astype(jnp.bfloat16)


def lane_block(rows, offset):
    return pl.BlockSpec((rows, PAIR), lambda p, h: (0, p + offset))


def attention_forward(q_arr, k_arr, v_arr, offsets, head_count, head_size, key_valid, vec=None, cut=None, prefix_blocks=0):
    q_count, key_count = q_arr.shape[0], k_arr.shape[0]
    self_mode = vec is not None
    per = PAIR // head_size
    pairs = head_count // per
    in_specs = [
        lane_block(q_count, offsets[0]),
        lane_block(key_count, offsets[1]),
        lane_block(key_count, offsets[2]),
    ]
    args = [q_arr, k_arr, v_arr]
    scratch = []
    if self_mode:
        lanes = vec.shape[-1]
        in_specs = [
            pl.BlockSpec(memory_space=pltpu.SMEM),
            pl.BlockSpec((1, 1, lanes), lambda p, h: (p * per + h, 0, 0)),
        ] + in_specs
        args = [cut, vec] + args
        scratch = [pltpu.VMEM((BLOCK, lanes), jnp.float32)]
    return pl.pallas_call(
        functools.partial(forward_kernel, self_mode, q_count, key_count, key_valid, head_size, prefix_blocks),
        out_shape=(
            jax.ShapeDtypeStruct((q_count, head_count * head_size), jnp.bfloat16),
            jax.ShapeDtypeStruct((q_count, head_count * head_size), jnp.bfloat16),
            jax.ShapeDtypeStruct((head_count, 1, q_count), jnp.float32),
        ),
        grid=(pairs, per),
        in_specs=in_specs,
        out_specs=(
            lane_block(q_count, 0),
            lane_block(q_count, 0),
            pl.BlockSpec((1, 1, q_count), lambda p, h: (p * per + h, 0, 0)),
        ),
        scratch_shapes=scratch,
        compiler_params=pltpu.CompilerParams(vmem_limit_bytes=40 << 20),
        cost_estimate=pl.CostEstimate(
            flops=4 * head_count * q_count * key_count * PAIR,
            bytes_accessed=4 * head_count * q_count * head_size * 2,
            transcendentals=head_count * q_count * key_count,
        ),
        name="self_forward" if self_mode else "cross_forward",
    )(*args)


def attention_backward(q_arr, k_arr, v_arr, offsets, out, rest, grad, log_total, head_count, head_size, key_valid, vec=None, cut=None, prefix_blocks=0):
    q_count, key_count = q_arr.shape[0], k_arr.shape[0]
    self_mode = vec is not None
    per = PAIR // head_size
    pairs = head_count // per
    width = head_count * head_size
    in_specs = [
        lane_block(q_count, offsets[0]),
        lane_block(key_count, offsets[1]),
        lane_block(key_count, offsets[2]),
        lane_block(q_count, 0),
        lane_block(q_count, 0),
        lane_block(q_count, 0),
        pl.BlockSpec((1, 1, q_count), lambda p, h: (p * per + h, 0, 0)),
    ]
    args = [q_arr, k_arr, v_arr, out, rest, grad, log_total]
    scratch = [
        pltpu.VMEM((PAIR, key_count), jnp.bfloat16),
        pltpu.VMEM((PAIR, q_count), jnp.float32),
        pltpu.VMEM((key_count, PAIR), jnp.float32),
        pltpu.VMEM((key_count, PAIR), jnp.float32),
    ]
    out_shape = [
        jax.ShapeDtypeStruct((q_count, width), jnp.bfloat16),
        jax.ShapeDtypeStruct((key_count, width), jnp.bfloat16),
        jax.ShapeDtypeStruct((key_count, width), jnp.bfloat16),
    ]
    out_specs = [lane_block(q_count, 0), lane_block(key_count, 0), lane_block(key_count, 0)]
    if self_mode:
        lanes = vec.shape[-1]
        in_specs = [
            pl.BlockSpec(memory_space=pltpu.SMEM),
            pl.BlockSpec((1, 1, lanes), lambda p, h: (p * per + h, 0, 0)),
        ] + in_specs
        args = [cut, vec] + args
        scratch += [pltpu.VMEM((BLOCK, lanes), jnp.float32), pltpu.VMEM((BLOCK, lanes), jnp.float32)]
        out_shape.append(jax.ShapeDtypeStruct((head_count, 8, lanes), jnp.float32))
        out_specs.append(pl.BlockSpec((1, 8, lanes), lambda p, h: (p * per + h, 0, 0)))
    return pl.pallas_call(
        functools.partial(backward_kernel, self_mode, q_count, key_count, key_valid, head_size, prefix_blocks),
        out_shape=tuple(out_shape),
        grid=(pairs, per),
        in_specs=in_specs,
        out_specs=tuple(out_specs),
        scratch_shapes=scratch,
        compiler_params=pltpu.CompilerParams(vmem_limit_bytes=40 << 20),
        cost_estimate=pl.CostEstimate(
            flops=10 * head_count * q_count * key_count * PAIR,
            bytes_accessed=8 * head_count * q_count * head_size * 2,
            transcendentals=head_count * q_count * key_count,
        ),
        name="self_backward" if self_mode else "cross_backward",
    )(*args)


def normalize(resid_rows, gain_vec):
    model_width = resid_rows.shape[1] * lax.axis_size("col")
    square_sum = lax.psum(jnp.sum(resid_rows * resid_rows, axis=1), "col")
    inv_scale = lax.rsqrt(square_sum / model_width + 1e-06)
    normed = lax.all_gather(
        (resid_rows * inv_scale[:, None] * gain_vec).astype(jnp.bfloat16), "col", axis=1, tiled=True
    )
    return (normed, inv_scale)


def norm_backward(grad_part, resid_rows, inv_scale, gain_vec):
    model_width = resid_rows.shape[1] * lax.axis_size("col")
    grad_normed = lax.psum_scatter(
        grad_part.astype(jnp.bfloat16), "col", scatter_dimension=1, tiled=True
    ).astype(jnp.float32)
    scaled = grad_normed * gain_vec
    inner_sum = lax.psum(jnp.sum(scaled * resid_rows, axis=1), "col")
    grad_resid = (
        inv_scale[:, None] * scaled
        - resid_rows * (inv_scale * inv_scale * inv_scale * inner_sum / model_width)[:, None]
    )
    grad_gain = jnp.sum(grad_normed * resid_rows * inv_scale[:, None], axis=0)
    return (grad_resid, grad_gain)


def branch_sum(partial_rows):
    return lax.psum_scatter(
        partial_rows.astype(jnp.bfloat16), "col", scatter_dimension=1, tiled=True
    ).astype(jnp.float32)


def branch_grad(grad_rows):
    return lax.all_gather(grad_rows.astype(jnp.bfloat16), "col", axis=1, tiled=True)


def body(
    residual_in,
    encoder_out,
    prefix_len,
    bucket_table,
    cotangent,
    norm_self,
    norm_cross,
    norm_ffn,
    self_query,
    self_key,
    self_value,
    self_out,
    cross_query,
    cross_key,
    cross_value,
    cross_out,
    ffn_in,
    ffn_out,
    rel_bias,
):
    low_type = jnp.bfloat16
    micro_count = residual_in.shape[0]
    seq_count = prefix_len.shape[1]
    seq_len = (bucket_table.shape[0] + 1) // 2
    token_rows = seq_count * seq_len
    head_count = rel_bias.shape[1]
    inner_width = self_query.shape[1]
    head_size = inner_width // head_count
    gathered = (
        lax.all_gather(self_query.astype(low_type), "row", axis=0, tiled=True),
        lax.all_gather(self_key.astype(low_type), "row", axis=0, tiled=True),
        lax.all_gather(self_value.astype(low_type), "row", axis=0, tiled=True),
        lax.all_gather(self_out.astype(low_type), "row", axis=1, tiled=True),
        lax.all_gather(cross_query.astype(low_type), "row", axis=0, tiled=True),
        lax.all_gather(cross_key.astype(low_type), "row", axis=0, tiled=True),
        lax.all_gather(cross_value.astype(low_type), "row", axis=0, tiled=True),
        lax.all_gather(cross_out.astype(low_type), "row", axis=1, tiled=True),
        lax.all_gather(ffn_in.astype(low_type), "row", axis=0, tiled=True),
        lax.all_gather(ffn_out.astype(low_type), "row", axis=1, tiled=True),
        lax.all_gather(rel_bias.astype(low_type), "row", axis=0, tiled=True),
    )
    full_self_query, full_self_key, full_self_value, full_self_out = (
        gathered[0],
        gathered[1],
        gathered[2],
        gathered[3],
    )
    full_cross_query, full_cross_key, full_cross_value, full_cross_out = (
        gathered[4],
        gathered[5],
        gathered[6],
        gathered[7],
    )
    full_ffn_in, full_ffn_out, full_bias = (gathered[8], gathered[9], gathered[10])
    model_width = full_self_query.shape[0]
    ffn_width = full_ffn_in.shape[1]
    qkv_weight = jnp.concatenate((full_self_query, full_self_key, full_self_value), axis=1)
    kv_weight = jnp.concatenate((full_cross_key, full_cross_value), axis=1)
    bucket_ids = jnp.arange(full_bias.shape[0], dtype=jnp.int32)
    bucket_onehot = (bucket_table[:, None] == bucket_ids[None, :]).astype(jnp.float32)
    distance_bias = jnp.dot(
        bucket_onehot, full_bias.astype(jnp.float32), precision=lax.Precision.HIGHEST
    ).T
    def band_rows(vector):
        return jnp.roll(jnp.pad(vector, ((0, 0), (0, 1))), 1 - BLOCK, axis=1)[:, None, :]

    band_forward = band_rows(distance_bias)
    band_backward = band_rows(distance_bias[:, ::-1])
    prefix_blocks = -(-(seq_len // 2) // BLOCK)
    pairs = head_count * head_size // PAIR

    outputs = []
    grad_inputs = []
    grad_memory = []
    running = [
        jnp.zeros((model_width, 3 * inner_width), jnp.float32),
        jnp.zeros((inner_width, model_width), jnp.float32),
        jnp.zeros((model_width, inner_width), jnp.float32),
        jnp.zeros((model_width, 2 * inner_width), jnp.float32),
        jnp.zeros((inner_width, model_width), jnp.float32),
        jnp.zeros((model_width, ffn_width), jnp.float32),
        jnp.zeros((ffn_width, model_width), jnp.float32),
        jnp.zeros((head_count, 8, 2 * seq_len), jnp.float32),
    ]
    gain_sums = [jnp.zeros(norm_self.shape, jnp.float32) for _ in range(3)]
    for micro_step in range(micro_count):
        resid_zero = residual_in[micro_step]
        normed_one, scale_one = normalize(resid_zero, norm_self)
        qkv_rows = project(normed_one, qkv_weight).astype(low_type)
        cut_len = prefix_len[micro_step]
        self_flat, self_rest, self_total = attention_forward(
            qkv_rows, qkv_rows, qkv_rows, (0, pairs, 2 * pairs), head_count, head_size, seq_len,
            band_forward, cut_len, prefix_blocks,
        )
        resid_one = resid_zero + branch_sum(project(self_flat, full_self_out))
        normed_two, scale_two = normalize(resid_one, norm_cross)
        cross_queries = project(normed_two, full_cross_query).astype(low_type)
        memory_rows = lax.all_gather(
            encoder_out[micro_step].astype(low_type), "col", axis=1, tiled=True
        )
        memory_len = memory_rows.shape[0]
        memory_rows = jnp.pad(memory_rows, ((0, -memory_len % BLOCK), (0, 0)))
        kv_rows = project(memory_rows, kv_weight).astype(low_type)
        cross_flat, cross_rest, cross_total = attention_forward(
            cross_queries, kv_rows, kv_rows, (0, 0, pairs), head_count, head_size, memory_len
        )
        resid_two = resid_one + branch_sum(project(cross_flat, full_cross_out))
        normed_three, scale_three = normalize(resid_two, norm_ffn)
        ffn_pre = project(normed_three, full_ffn_in)
        act_values, act_pull = jax.vjp(smooth_act, ffn_pre)
        ffn_act = act_values.astype(low_type)
        outputs.append(resid_two + branch_sum(project(ffn_act, full_ffn_out)))
        grad_top = cotangent[micro_step]
        grad_rows = branch_grad(grad_top)
        running[6] = running[6] + project_left(ffn_act, grad_rows)
        grad_pre = act_pull(project_back(grad_rows, full_ffn_out))[0].astype(low_type)
        running[5] = running[5] + project_left(normed_three, grad_pre)
        grad_two, gain_part = norm_backward(
            project_back(grad_pre, full_ffn_in), resid_two, scale_three, norm_ffn
        )
        gain_sums[2] = gain_sums[2] + gain_part
        grad_two = grad_two + grad_top
        grad_rows = branch_grad(grad_two)
        running[4] = running[4] + project_left(cross_flat, grad_rows)
        grad_cross_mix = project_back(grad_rows, full_cross_out).astype(low_type)
        cross_grad_flat, cross_grad_key, cross_grad_value = attention_backward(
            cross_queries, kv_rows, kv_rows, (0, 0, pairs), cross_flat, cross_rest, grad_cross_mix, cross_total,
            head_count, head_size, memory_len,
        )
        grad_kv = jnp.concatenate((cross_grad_key, cross_grad_value), axis=1)
        running[2] = running[2] + project_left(normed_two, cross_grad_flat)
        running[3] = running[3] + project_left(memory_rows, grad_kv)
        grad_memory.append(
            lax.psum_scatter(
                project_back(grad_kv, kv_weight)[:memory_len].astype(jnp.bfloat16),
                "col",
                scatter_dimension=1,
                tiled=True,
            ).astype(jnp.float32)
        )
        grad_one, gain_part = norm_backward(
            project_back(cross_grad_flat, full_cross_query), resid_one, scale_two, norm_cross
        )
        gain_sums[1] = gain_sums[1] + gain_part
        grad_one = grad_one + grad_two
        grad_rows = branch_grad(grad_one)
        running[1] = running[1] + project_left(self_flat, grad_rows)
        grad_self_mix = project_back(grad_rows, full_self_out).astype(low_type)
        self_grad_query, self_grad_key, self_grad_value, diag_part = attention_backward(
            qkv_rows, qkv_rows, qkv_rows, (0, pairs, 2 * pairs), self_flat, self_rest, grad_self_mix, self_total,
            head_count, head_size, seq_len, band_backward, cut_len, prefix_blocks,
        )
        running[7] = running[7] + diag_part
        grad_qkv = jnp.concatenate((self_grad_query, self_grad_key, self_grad_value), axis=1)
        running[0] = running[0] + project_left(normed_one, grad_qkv)
        grad_zero, gain_part = norm_backward(
            project_back(grad_qkv, qkv_weight), resid_zero, scale_one, norm_self
        )
        gain_sums[0] = gain_sums[0] + gain_part
        grad_inputs.append(grad_zero + grad_one)
    diagonals = sum(jnp.roll(running[7][:, row], -row, axis=1) for row in range(8))
    place_onehot = jnp.roll(
        jnp.pad(bucket_onehot[::-1], ((0, 1), (0, 0))), 1 - BLOCK, axis=0
    )
    bias_grad = jnp.dot(place_onehot.T, diagonals.T, precision=lax.Precision.HIGHEST)
    weight_grads = (
        lax.psum_scatter(
            running[0][:, :inner_width].astype(jnp.bfloat16),
            ("dp", "row"),
            scatter_dimension=0,
            tiled=True,
        ).astype(jnp.float32),
        lax.psum_scatter(
            running[0][:, inner_width : 2 * inner_width].astype(jnp.bfloat16),
            ("dp", "row"),
            scatter_dimension=0,
            tiled=True,
        ).astype(jnp.float32),
        lax.psum_scatter(
            running[0][:, 2 * inner_width :].astype(jnp.bfloat16),
            ("dp", "row"),
            scatter_dimension=0,
            tiled=True,
        ).astype(jnp.float32),
        lax.psum_scatter(
            running[1].astype(jnp.bfloat16), ("dp", "row"), scatter_dimension=1, tiled=True
        ).astype(jnp.float32),
        lax.psum_scatter(
            running[2].astype(jnp.bfloat16), ("dp", "row"), scatter_dimension=0, tiled=True
        ).astype(jnp.float32),
        lax.psum_scatter(
            running[3][:, :inner_width].astype(jnp.bfloat16),
            ("dp", "row"),
            scatter_dimension=0,
            tiled=True,
        ).astype(jnp.float32),
        lax.psum_scatter(
            running[3][:, inner_width:].astype(jnp.bfloat16),
            ("dp", "row"),
            scatter_dimension=0,
            tiled=True,
        ).astype(jnp.float32),
        lax.psum_scatter(
            running[4].astype(jnp.bfloat16), ("dp", "row"), scatter_dimension=1, tiled=True
        ).astype(jnp.float32),
        lax.psum_scatter(
            running[5].astype(jnp.bfloat16), ("dp", "row"), scatter_dimension=0, tiled=True
        ).astype(jnp.float32),
        lax.psum_scatter(
            running[6].astype(jnp.bfloat16), ("dp", "row"), scatter_dimension=1, tiled=True
        ).astype(jnp.float32),
        lax.psum_scatter(
            bias_grad.astype(jnp.bfloat16), ("dp", "row"), scatter_dimension=0, tiled=True
        ).astype(jnp.float32),
    )
    gain_grads = lax.psum((gain_sums[0], gain_sums[1], gain_sums[2]), ("dp", "row"))
    return (
        jnp.stack(outputs),
        jnp.stack(grad_inputs),
        jnp.stack(grad_memory),
        gain_grads[0],
        gain_grads[1],
        gain_grads[2],
        weight_grads[0],
        weight_grads[1],
        weight_grads[2],
        weight_grads[3],
        weight_grads[4],
        weight_grads[5],
        weight_grads[6],
        weight_grads[7],
        weight_grads[8],
        weight_grads[9],
        weight_grads[10],
    )


def solution(mesh):
    in_specs = (
        P(None, ("dp", "row"), "col"),
        P(None, ("dp", "row"), "col"),
        P(None, ("dp", "row")),
        P(),
        P(None, ("dp", "row"), "col"),
        P("col"),
        P("col"),
        P("col"),
        P("row", "col"),
        P("row", "col"),
        P("row", "col"),
        P("col", "row"),
        P("row", "col"),
        P("row", "col"),
        P("row", "col"),
        P("col", "row"),
        P("row", "col"),
        P("col", "row"),
        P("row", "col"),
    )
    out_specs = (
        P(None, ("dp", "row"), "col"),
        P(None, ("dp", "row"), "col"),
        P(None, ("dp", "row"), "col"),
        P("col"),
        P("col"),
        P("col"),
        P(("dp", "row"), "col"),
        P(("dp", "row"), "col"),
        P(("dp", "row"), "col"),
        P("col", ("dp", "row")),
        P(("dp", "row"), "col"),
        P(("dp", "row"), "col"),
        P(("dp", "row"), "col"),
        P("col", ("dp", "row")),
        P(("dp", "row"), "col"),
        P("col", ("dp", "row")),
        P(("dp", "row"), "col"),
    )
    return jax.shard_map(body, mesh=mesh, in_specs=in_specs, out_specs=out_specs, check_vma=False)
```

```python
import functools

import jax
import jax.numpy as jnp
from jax import lax
from jax.experimental import pallas as pl
from jax.experimental.pallas import tpu as pltpu
from jax.sharding import PartitionSpec as P

NEG_FILL = -1000000000.0
BLOCK = 256
PAIR = 128
LOW = jnp.bfloat16
WIDE = jnp.float32


def dot_tn(left, right):
    return lax.dot_general(left, right, (((0,), (0,)), ((), ())), preferred_element_type=jnp.float32)


def dot_nt(left, right):
    return lax.dot_general(left, right, (((1,), (1,)), ((), ())), preferred_element_type=jnp.float32)


def dot_nn(left, right):
    return lax.dot_general(left, right, (((1,), (0,)), ((), ())), preferred_element_type=jnp.float32)


def head_mask(head, head_size):
    lane = lax.broadcasted_iota(jnp.int32, (1, PAIR), 1)
    low = head * head_size
    return ((lane >= low) & (lane < low + head_size)).astype(jnp.float32)


def key_blocks(q_block, key_count, self_mode, prefix_blocks):
    total = key_count // BLOCK
    return min(total, max(q_block + 1, prefix_blocks)) if self_mode else total


def forward_kernel(self_mode, q_count, key_count, key_valid, head_size, prefix_blocks, *refs):
    if self_mode:
        cut_ref, vec_ref, q_ref, k_ref, v_ref, o_ref, rest_ref, lse_ref, band = refs
    else:
        q_ref, k_ref, v_ref, o_ref, rest_ref, lse_ref = refs
    head = pl.program_id(1)
    mask = head_mask(head, head_size)
    mask_low = mask.astype(jnp.bfloat16)
    if self_mode:
        wide = jnp.broadcast_to(vec_ref[0], (BLOCK, band.shape[1]))
        band[...] = pltpu.roll(wide, 0, 1, stride=1, stride_axis=0)
        cut = cut_ref[0]
    base = q_count - BLOCK
    col = lax.broadcasted_iota(jnp.int32, (BLOCK, BLOCK), 1)
    row = lax.broadcasted_iota(jnp.int32, (BLOCK, BLOCK), 0)
    for qb in range(q_count // BLOCK):
        q_rows = pl.ds(qb * BLOCK, BLOCK)
        query = q_ref[q_rows, :] * mask_low
        parts = []
        for kb in range(key_blocks(qb, key_count, self_mode, prefix_blocks)):
            s = dot_nt(query, k_ref[pl.ds(kb * BLOCK, BLOCK), :])
            if self_mode:
                s = s + band[:, pl.ds((kb - qb) * BLOCK + base, BLOCK)]
                if kb >= qb:
                    limit = jnp.maximum(row + qb * BLOCK, cut - 1)
                    s = jnp.where(col + kb * BLOCK <= limit, s, NEG_FILL)
            elif (kb + 1) * BLOCK > key_valid:
                s = jnp.where(col + kb * BLOCK < key_valid, s, NEG_FILL)
            parts.append(s)
        top = functools.reduce(jnp.maximum, [jnp.max(s, axis=1, keepdims=True) for s in parts])
        total = jnp.zeros((BLOCK, 1), jnp.float32)
        mixed = jnp.zeros((BLOCK, PAIR), jnp.float32)
        for kb, s in enumerate(parts):
            e = jnp.exp(s - top)
            total = total + jnp.sum(e, axis=1, keepdims=True)
            mixed = mixed + dot_nn(e.astype(jnp.bfloat16), v_ref[pl.ds(kb * BLOCK, BLOCK), :])
        mixed = mixed * (mask / total)
        mixed_low = mixed.astype(jnp.bfloat16)
        rest = (mixed - mixed_low.astype(jnp.float32)).astype(jnp.bfloat16)

        @pl.when(head == 0)
        def _():
            o_ref[q_rows, :] = mixed_low
            rest_ref[q_rows, :] = rest

        @pl.when(head > 0)
        def _():
            o_ref[q_rows, :] += mixed_low
            rest_ref[q_rows, :] += rest

        log_total = jnp.broadcast_to(top + jnp.log(total), (BLOCK, PAIR))
        lse_ref[0, :, q_rows] = log_total.T[:1]


def backward_kernel(self_mode, q_count, key_count, key_valid, head_size, prefix_blocks, *refs):
    if self_mode:
        cut_ref, vec_ref, q_ref, k_ref, v_ref, o_ref, rest_ref, do_ref, lse_ref = refs[:9]
        dq_ref, dk_ref, dv_ref, diag_ref, kt, dqt, dk_acc, dv_acc, band, acc = refs[9:]
    else:
        q_ref, k_ref, v_ref, o_ref, rest_ref, do_ref, lse_ref = refs[:7]
        dq_ref, dk_ref, dv_ref, kt, dqt, dk_acc, dv_acc = refs[7:]
    head = pl.program_id(1)
    mask = head_mask(head, head_size)
    mask_low = mask.astype(jnp.bfloat16)
    base = q_count - BLOCK

    @pl.when(head == 0)
    def _():
        kt[...] = k_ref[...].T
        dk_acc[...] = jnp.zeros_like(dk_acc)
        dv_acc[...] = jnp.zeros_like(dv_acc)

    if self_mode:
        wide = jnp.broadcast_to(vec_ref[0], (BLOCK, band.shape[1]))
        band[...] = pltpu.roll(wide, 0, 1, stride=1, stride_axis=0)
        acc[...] = jnp.zeros_like(acc)
        cut = cut_ref[0]
    col = lax.broadcasted_iota(jnp.int32, (BLOCK, BLOCK), 1)
    row = lax.broadcasted_iota(jnp.int32, (BLOCK, BLOCK), 0)
    head_rows = pl.ds(pl.multiple_of(head * head_size, head_size), head_size)
    key_t = kt[head_rows, :]
    for qb in range(q_count // BLOCK):
        q_rows = pl.ds(qb * BLOCK, BLOCK)
        query = q_ref[q_rows, :] * mask_low
        grad = do_ref[q_rows, :] * mask_low
        mixed = o_ref[q_rows, :].astype(jnp.float32) + rest_ref[q_rows, :].astype(jnp.float32)
        product = grad.astype(jnp.float32) * mixed
        delta = jnp.sum(product.T, axis=0, keepdims=True)
        log_total = lse_ref[0, :, q_rows]
        dqt_sum = jnp.zeros((head_size, BLOCK), jnp.float32)
        for kb in range(key_blocks(qb, key_count, self_mode, prefix_blocks)):
            k_rows = pl.ds(kb * BLOCK, BLOCK)
            s = dot_nt(k_ref[k_rows, :], query)
            dp = dot_nt(v_ref[k_rows, :], grad)
            if self_mode:
                span = pl.ds((qb - kb) * BLOCK + base, BLOCK)
                s = s + band[:, span]
                if kb >= qb:
                    limit = jnp.maximum(col + qb * BLOCK, cut - 1)
                    s = jnp.where(row + kb * BLOCK <= limit, s, NEG_FILL)
            elif (kb + 1) * BLOCK > key_valid:
                s = jnp.where(row + kb * BLOCK < key_valid, s, NEG_FILL)
            p = jnp.exp(s - log_total)
            ds = p * (dp - delta)
            ds_low = ds.astype(jnp.bfloat16)
            if self_mode:
                acc[:, span] += ds
            dv_acc[k_rows, :] += dot_nn(p.astype(jnp.bfloat16), grad)
            dk_acc[k_rows, :] += dot_nn(ds_low, query)
            dqt_sum = dqt_sum + dot_nn(key_t[:, kb * BLOCK : (kb + 1) * BLOCK], ds_low)
        dqt[head_rows, q_rows] = dqt_sum
    if self_mode:
        size = BLOCK
        fold = acc[...]
        lanes = fold.shape[1]
        while size > 8:
            size //= 2
            fold = fold[:size] + pltpu.roll(fold[size:], lanes - size, 1)
        diag_ref[0] = fold

    @pl.when(head == pl.num_programs(1) - 1)
    def _():
        dq_ref[...] = dqt[...].T.astype(jnp.bfloat16)
        dk_ref[...] = dk_acc[...].astype(jnp.bfloat16)
        dv_ref[...] = dv_acc[...].astype(jnp.bfloat16)


def lane_block(rows, offset):
    return pl.BlockSpec((rows, PAIR), lambda p, h: (0, p + offset))


def attention_forward(q_arr, k_arr, v_arr, offsets, head_count, head_size, key_valid, vec=None, cut=None, prefix_blocks=0):
    q_count, key_count = q_arr.shape[0], k_arr.shape[0]
    self_mode = vec is not None
    per = PAIR // head_size
    pairs = head_count // per
    in_specs = [
        lane_block(q_count, offsets[0]),
        lane_block(key_count, offsets[1]),
        lane_block(key_count, offsets[2]),
    ]
    args = [q_arr, k_arr, v_arr]
    scratch = []
    if self_mode:
        lanes = vec.shape[-1]
        in_specs = [
            pl.BlockSpec(memory_space=pltpu.SMEM),
            pl.BlockSpec((1, 1, lanes), lambda p, h: (p * per + h, 0, 0)),
        ] + in_specs
        args = [cut, vec] + args
        scratch = [pltpu.VMEM((BLOCK, lanes), jnp.float32)]
    return pl.pallas_call(
        functools.partial(forward_kernel, self_mode, q_count, key_count, key_valid, head_size, prefix_blocks),
        out_shape=(
            jax.ShapeDtypeStruct((q_count, head_count * head_size), jnp.bfloat16),
            jax.ShapeDtypeStruct((q_count, head_count * head_size), jnp.bfloat16),
            jax.ShapeDtypeStruct((head_count, 1, q_count), jnp.float32),
        ),
        grid=(pairs, per),
        in_specs=in_specs,
        out_specs=(
            lane_block(q_count, 0),
            lane_block(q_count, 0),
            pl.BlockSpec((1, 1, q_count), lambda p, h: (p * per + h, 0, 0)),
        ),
        scratch_shapes=scratch,
        compiler_params=pltpu.CompilerParams(vmem_limit_bytes=40 << 20),
        cost_estimate=pl.CostEstimate(
            flops=4 * head_count * q_count * key_count * PAIR,
            bytes_accessed=4 * head_count * q_count * head_size * 2,
            transcendentals=head_count * q_count * key_count,
        ),
        name="self_forward" if self_mode else "cross_forward",
    )(*args)


def attention_backward(q_arr, k_arr, v_arr, offsets, out, rest, grad, log_total, head_count, head_size, key_valid, vec=None, cut=None, prefix_blocks=0):
    q_count, key_count = q_arr.shape[0], k_arr.shape[0]
    self_mode = vec is not None
    per = PAIR // head_size
    pairs = head_count // per
    width = head_count * head_size
    in_specs = [
        lane_block(q_count, offsets[0]),
        lane_block(key_count, offsets[1]),
        lane_block(key_count, offsets[2]),
        lane_block(q_count, 0),
        lane_block(q_count, 0),
        lane_block(q_count, 0),
        pl.BlockSpec((1, 1, q_count), lambda p, h: (p * per + h, 0, 0)),
    ]
    args = [q_arr, k_arr, v_arr, out, rest, grad, log_total]
    scratch = [
        pltpu.VMEM((PAIR, key_count), jnp.bfloat16),
        pltpu.VMEM((PAIR, q_count), jnp.float32),
        pltpu.VMEM((key_count, PAIR), jnp.float32),
        pltpu.VMEM((key_count, PAIR), jnp.float32),
    ]
    out_shape = [
        jax.ShapeDtypeStruct((q_count, width), jnp.bfloat16),
        jax.ShapeDtypeStruct((key_count, width), jnp.bfloat16),
        jax.ShapeDtypeStruct((key_count, width), jnp.bfloat16),
    ]
    out_specs = [lane_block(q_count, 0), lane_block(key_count, 0), lane_block(key_count, 0)]
    if self_mode:
        lanes = vec.shape[-1]
        in_specs = [
            pl.BlockSpec(memory_space=pltpu.SMEM),
            pl.BlockSpec((1, 1, lanes), lambda p, h: (p * per + h, 0, 0)),
        ] + in_specs
        args = [cut, vec] + args
        scratch += [pltpu.VMEM((BLOCK, lanes), jnp.float32), pltpu.VMEM((BLOCK, lanes), jnp.float32)]
        out_shape.append(jax.ShapeDtypeStruct((head_count, 8, lanes), jnp.float32))
        out_specs.append(pl.BlockSpec((1, 8, lanes), lambda p, h: (p * per + h, 0, 0)))
    return pl.pallas_call(
        functools.partial(backward_kernel, self_mode, q_count, key_count, key_valid, head_size, prefix_blocks),
        out_shape=tuple(out_shape),
        grid=(pairs, per),
        in_specs=in_specs,
        out_specs=tuple(out_specs),
        scratch_shapes=scratch,
        compiler_params=pltpu.CompilerParams(vmem_limit_bytes=40 << 20),
        cost_estimate=pl.CostEstimate(
            flops=10 * head_count * q_count * key_count * PAIR,
            bytes_accessed=8 * head_count * q_count * head_size * 2,
            transcendentals=head_count * q_count * key_count,
        ),
        name="self_backward" if self_mode else "cross_backward",
    )(*args)


def smooth_act(values):
    return jax.nn.gelu(values, approximate=True)


class Layout:
    def __init__(self):
        self.col = lax.axis_size("col")
        self.team = self.col // 2
        self.bits = self.team.bit_length() - 1
        self.rows = lax.axis_size("row")
        self.index = lax.axis_index("col")
        self.micro = self.index // self.team
        self.member = self.index % self.team
        self.dp = lax.axis_index("dp")
        self.row = lax.axis_index("row")
        self.far_index = (1 - self.micro) * self.team + self.member

    def swap_half(self, array):
        return lax.ppermute(array, "col", [(i, (i + self.team) % self.col) for i in range(self.col)])

    def swap_bit(self, array, bit):
        return lax.ppermute(array, "col", [(i, i ^ (1 << bit)) for i in range(self.col)])

    def swap_dp(self, array):
        return lax.ppermute(array, "dp", [(0, 1), (1, 0)])

    def swap_row(self, array, bit):
        return lax.ppermute(array, "row", [(i, i ^ (1 << bit)) for i in range(self.rows)])

    def bit_of(self, bit):
        return (self.member >> bit) & 1

    def own(self, pair):
        return jnp.where(self.micro == 0, pair[0], pair[1])

    def other(self, pair):
        return jnp.where(self.micro == 0, pair[1], pair[0])

    def in_order(self, own, other):
        return jnp.stack((jnp.where(self.micro == 0, own, other), jnp.where(self.micro == 0, other, own)))

    def team_gather(self, array):
        parts = [array]
        for bit in range(self.bits):
            sent = parts[0] if len(parts) == 1 else jnp.stack(parts)
            got = self.swap_bit(sent, bit)
            got = [got] if len(parts) == 1 else [got[i] for i in range(len(parts))]
            low = self.bit_of(bit) == 0
            parts = [jnp.where(low, mine, far) for mine, far in zip(parts, got)] + [
                jnp.where(low, far, mine) for mine, far in zip(parts, got)
            ]
        return parts

    def team_sum(self, array):
        for bit in range(self.bits):
            array = array + self.swap_bit(array.astype(LOW), bit).astype(WIDE)
        return array

    def team_scatter(self, arrays, axis, kind=LOW):
        for bit in reversed(range(self.bits)):
            half = arrays[0].shape[axis] // 2
            mine = self.bit_of(bit)
            keep = [lax.dynamic_slice_in_dim(a, mine * half, half, axis) for a in arrays]
            sent = [lax.dynamic_slice_in_dim(a, (1 - mine) * half, half, axis) for a in arrays]
            got = self.swap_bit(jnp.concatenate(sent).astype(kind), bit).astype(WIDE)
            starts = [sum(k.shape[0] for k in keep[:i]) for i in range(len(keep))]
            arrays = [k + got[at : at + k.shape[0]] for k, at in zip(keep, starts)]
        return arrays

    def half_columns(self, array):
        size = array.shape[1] // 2
        return [
            lax.dynamic_slice_in_dim(array, start * size, size, 1)
            for start in (self.micro, 1 - self.micro)
        ]

    def full_width(self, own, other):
        low, high = jnp.where(self.micro == 0, own, other), jnp.where(self.micro == 0, other, own)
        parts = self.team_gather(jnp.stack((low, high)))
        return jnp.concatenate([part[half] for half in range(2) for part in parts], axis=1)

    def sum_rows(self, array):
        half = array.shape[0] // 2
        keep = lax.dynamic_slice_in_dim(array, self.dp * half, half, 0)
        sent = lax.dynamic_slice_in_dim(array, (1 - self.dp) * half, half, 0)
        array = keep.astype(WIDE) + self.swap_dp(sent.astype(LOW)).astype(WIDE)
        columns = array.shape[1]
        bits = self.rows.bit_length() - 1
        for bit in range(bits):
            left = 1 << (bits - bit - 1)
            pieces = array.reshape(left, 2, -1, columns)
            mine = (self.row >> bit) & 1
            keep = lax.dynamic_index_in_dim(pieces, mine, 1, keepdims=False)
            sent = lax.dynamic_index_in_dim(pieces, 1 - mine, 1, keepdims=False)
            array = keep + self.swap_row(sent.astype(LOW), bit).astype(WIDE)
            array = array.reshape(-1, columns)
        return array

    def sum_all(self, array):
        array = array + self.swap_dp(array)
        for bit in range(self.rows.bit_length() - 1):
            array = array + self.swap_row(array, bit)
        return array


def tie(*arrays):
    return lax.optimization_barrier(arrays)


def rms(rows):
    return lax.rsqrt(jnp.mean(rows * rows, axis=1, keepdims=True) + 1e-06)


def norm_backward(grad, rows, scale, gain):
    scaled = grad * gain
    inner = jnp.mean(scaled * rows, axis=1, keepdims=True)
    return scale * scaled - rows * (scale * scale * scale * inner)


def gain_part(grad, rows, scale):
    return jnp.sum(grad * (rows * scale), axis=0)


def body(
    residual_in,
    encoder_out,
    prefix_len,
    bucket_table,
    cotangent,
    norm_self,
    norm_cross,
    norm_ffn,
    self_query,
    self_key,
    self_value,
    self_out,
    cross_query,
    cross_key,
    cross_value,
    cross_out,
    ffn_in,
    ffn_out,
    rel_bias,
):
    place = Layout()
    team = place.team
    micro_count, rows, width = residual_in.shape
    assert micro_count == 2 and prefix_len.shape[1] == 1 and lax.axis_size("dp") == 2
    memory_len = encoder_out.shape[1]
    heads = rel_bias.shape[1]
    inner = self_query.shape[1]
    head_size = inner // heads
    units = ffn_in.shape[1]
    bias_rows = rel_bias.shape[0]
    buckets = bias_rows * place.rows
    pairs = inner // PAIR
    model = width * place.col
    cut = place.own(prefix_len)

    resid_low = residual_in.astype(LOW)
    resid_far = place.swap_half(place.other(resid_low))
    resid = place.full_width(place.own(resid_low), resid_far).astype(WIDE)
    gain_own = jnp.stack((norm_self, norm_cross, norm_ffn))
    gain_full = place.full_width(gain_own, place.swap_half(gain_own))
    gains = [gain_full[i : i + 1] for i in range(3)]

    def gather_half(blocks, extra=None):
        local = jnp.concatenate([block.astype(LOW) for block in blocks], axis=1)
        half = local.shape[0] // 2
        mine = jnp.where(place.dp == 0, local[:half], local[half:])
        if extra is not None:
            mine = jnp.concatenate((mine, extra))
        return lax.all_gather(mine, "row", axis=0, tiled=True)

    def join(first, second):
        count = model // (2 * place.rows)
        first, second = (a.reshape(place.rows, -1, a.shape[1])[:, :count] for a in (first, second))
        low = jnp.where(place.dp == 0, first, second)
        high = jnp.where(place.dp == 0, second, first)
        return jnp.concatenate((low, high), axis=1).reshape(model, -1)

    spare = jnp.pad(rel_bias.reshape(-1), (0, 8 * 3 * inner - rel_bias.size)).astype(LOW)
    near = gather_half((self_query, self_key, self_value), spare.reshape(8, -1))
    far = place.swap_half(near)
    qkv_weights = [join(near, place.swap_dp(near)), join(far, place.swap_dp(far))]
    tables = [
        side.reshape(place.rows, -1, 3 * inner)[:, -8:].reshape(place.rows, -1)[:, : rel_bias.size]
        .reshape(buckets, heads).astype(WIDE)
        for side in (near, far)
    ]
    mid_near = gather_half((self_out.T, cross_query, cross_key, cross_value, cross_out.T))
    mid_far = place.swap_half(mid_near)
    mid_weights = [join(mid_near, place.swap_dp(mid_near)), join(mid_far, place.swap_dp(mid_far))]
    out_weights = [w[:, :inner] for w in mid_weights]
    cross_q_weights = [w[:, inner : 2 * inner] for w in mid_weights]
    cross_kv_weights = [w[:, 2 * inner : 4 * inner] for w in mid_weights]
    cross_out_weights = [w[:, 4 * inner :] for w in mid_weights]
    ffn_near = gather_half((ffn_in, ffn_out.T))

    bucket_ids = jnp.arange(buckets, dtype=jnp.int32)

    def onehot(index):
        index = jnp.roll(jnp.pad(index, (0, 1), constant_values=-1), 1 - BLOCK)
        return (index[:, None] == bucket_ids[None, :]).astype(WIDE)

    def bands(index):
        return [
            jnp.dot(index, table, precision=lax.Precision.HIGHEST).T.reshape(heads, 1, -1)
            for table in tables
        ]

    back_onehot = onehot(bucket_table[::-1])
    bands_forward = bands(onehot(bucket_table))
    bands_backward = bands(back_onehot)
    prefix_blocks = -(-(rows // 2) // BLOCK)

    memory_low = encoder_out.astype(LOW)
    memory_far = place.swap_half(place.other(memory_low))
    memory = place.full_width(place.own(memory_low), memory_far)
    memory = jnp.pad(memory, ((0, -memory_len % BLOCK), (0, 0)))
    cot_low = cotangent.astype(LOW)
    cot_far = place.swap_half(cot_low)

    scale_one = rms(resid)
    normed_one = (resid * scale_one * gains[0]).astype(LOW)
    qkv, self_mix = [], []
    for weight, band in zip(qkv_weights, bands_forward):
        qkv.append(dot_nn(normed_one, weight).astype(LOW))
        self_mix.append(
            attention_forward(
                qkv[-1], qkv[-1], qkv[-1], (0, pairs, 2 * pairs), heads, head_size, rows, band, cut,
                prefix_blocks,
            )
        )
    part = sum(dot_nt(mix[0], w) for mix, w in zip(self_mix, out_weights))
    part, ffn_near, memory = tie(part, ffn_near, memory)
    added = place.team_sum(part)
    resid_one = resid + added
    ffn_far = place.swap_dp(ffn_near)

    scale_two = rms(resid_one)
    normed_two = (resid_one * scale_two * gains[1]).astype(LOW)
    cross_q, cross_kv, cross_mix = [], [], []
    for q_weight, kv_weight in zip(cross_q_weights, cross_kv_weights):
        cross_kv.append(dot_nn(memory, kv_weight).astype(LOW))
        cross_q.append(dot_nn(normed_two, q_weight).astype(LOW))
        cross_mix.append(
            attention_forward(
                cross_q[-1], cross_kv[-1], cross_kv[-1], (0, 0, pairs), heads, head_size, memory_len
            )
        )
    part = sum(dot_nt(mix[0], w) for mix, w in zip(cross_mix, cross_out_weights))
    part, ffn_far, cot_far = tie(part, ffn_far, cot_far)
    added_two = place.team_sum(part)
    added = added + added_two
    resid_two = resid_one + added_two
    cot_own = place.full_width(place.own(cot_low), place.own(cot_far))
    cot_other = place.full_width(place.other(cot_low), place.other(cot_far))

    ffn_weights = join(ffn_near, ffn_far)
    weight_in, weight_out = ffn_weights[:, :units], ffn_weights[:, units:]
    scale_three = rms(resid_two)
    normed_three = (resid_two * scale_three * gains[2]).astype(LOW)
    chunk = rows // team
    sent = lax.dynamic_slice_in_dim(normed_three, place.member * chunk, chunk, axis=0)
    got = place.swap_half(sent)

    def feed_forward(normed, cot):
        act_values, act_pull = jax.vjp(smooth_act, dot_nn(normed, weight_in))
        return act_values.astype(LOW), act_pull(dot_nn(cot, weight_out))[0].astype(LOW)

    act_own, pre_own = feed_forward(normed_three, cot_own)
    got, act_own, pre_own = tie(got, act_own, pre_own)
    far_three = jnp.concatenate(place.team_gather(got))
    act_other, pre_other = feed_forward(far_three, cot_other)
    (piece,) = place.team_scatter([dot_nt(pre_other, weight_in)], 0)
    got = place.swap_half(piece.astype(LOW))
    (piece,) = place.team_scatter([dot_nt(pre_own, weight_in)], 0)

    def reduce_rows(array):
        return lax.psum_scatter(array.astype(LOW), ("dp", "row"), scatter_dimension=0, tiled=True)

    ffn_pack = jnp.concatenate(
        (
            dot_tn(normed_three, pre_own) + dot_tn(far_three, pre_other),
            dot_tn(cot_own, act_own) + dot_tn(cot_other, act_other),
        ),
        axis=1,
    ).astype(LOW)
    tops = [dot_nt(act, weight_out) for act in (act_own, act_other)]
    got, ffn_pack, *tops = tie(got, ffn_pack, *tops)
    grad_three = place.team_gather((piece + got.astype(WIDE)).astype(LOW))
    grad_three = jnp.concatenate(grad_three).astype(WIDE)
    ffn_grads = reduce_rows(ffn_pack)

    gain_three = gain_part(grad_three, resid_two, scale_three)
    grad_two = norm_backward(grad_three, resid_two, scale_three, gains[2])
    grad_low = (cot_own.astype(WIDE) + grad_two).astype(LOW)

    columns = [part for top in tops for part in place.half_columns(top)]
    own_keep, own_send, other_keep, other_send = place.team_scatter(columns, 1)
    own_keep = own_keep + lax.dynamic_slice_in_dim(added, place.index * width, width, 1)
    own_send = own_send + lax.dynamic_slice_in_dim(added, place.far_index * width, width, 1)
    top_got = place.swap_half(jnp.stack((other_send, own_send)).astype(LOW))

    cross_grads = [None, None]
    cross_packs = [None, None]
    cross_got = None
    for side in (1, 0):
        mix, rest, log_total = cross_mix[side]
        grad_mix = dot_nn(grad_low, cross_out_weights[side]).astype(LOW)
        dq, dk, dv = attention_backward(
            cross_q[side], cross_kv[side], cross_kv[side], (0, 0, pairs), mix, rest, grad_mix,
            log_total, heads, head_size, memory_len,
        )
        if side == 0:
            dq, top_got = tie(dq, top_got)
        cross_grads[side] = (dq, jnp.concatenate((dk, dv), axis=1))
        cross_packs[side] = jnp.concatenate(
            (
                dot_tn(normed_two, dq),
                dot_tn(memory, cross_grads[side][1]),
                dot_tn(grad_low, mix),
            ),
            axis=1,
        ).astype(LOW)
        if side == 1:
            cross_got = place.swap_half(cross_packs[1])
    layer_out = residual_in + place.in_order(
        own_keep + top_got[0].astype(WIDE), other_keep + top_got[1].astype(WIDE)
    )
    grad_part = sum(dot_nt(cross_grads[side][0], cross_q_weights[side]) for side in (1, 0))
    memory_part = sum(dot_nt(cross_grads[side][1], cross_kv_weights[side]) for side in (1, 0))
    gain_two = gain_part(grad_part, resid_one, scale_two)
    grad_one = grad_two + norm_backward(
        place.team_sum(grad_part), resid_one, scale_two, gains[1]
    )

    grad_low = (cot_own.astype(WIDE) + grad_one).astype(LOW)
    cross_got, grad_low = tie(cross_got, grad_low)
    cross_total = reduce_rows(cross_packs[0].astype(WIDE) + cross_got.astype(WIDE))
    memory_keep, memory_send = place.team_scatter(place.half_columns(memory_part), 1)
    memory_got = place.swap_half(memory_send[:memory_len].astype(LOW))
    self_grads = [None, None]
    out_packs = [dot_tn(grad_low, mix[0]).astype(LOW) for mix in self_mix]
    out_got = place.swap_half(out_packs[1])
    self_packs = [None, None]
    diagonals = [None, None]
    for side in (1, 0):
        mix, rest, log_total = self_mix[side]
        grad_mix = dot_nn(grad_low, out_weights[side]).astype(LOW)
        dq, dk, dv, diagonals[side] = attention_backward(
            qkv[side], qkv[side], qkv[side], (0, pairs, 2 * pairs), mix, rest, grad_mix,
            log_total, heads, head_size, rows, bands_backward[side], cut, prefix_blocks,
        )
        if side == 0:
            dq, self_got, out_got, memory_got = tie(dq, self_got, out_got, memory_got)
        self_grads[side] = jnp.concatenate((dq, dk, dv), axis=1)
        self_packs[side] = dot_tn(normed_one, self_grads[side]).astype(LOW)
        if side == 1:
            self_got = place.swap_half(self_packs[1])
    grad_memory = place.in_order(memory_keep[:memory_len], memory_got.astype(WIDE))
    self_total = jnp.concatenate(
        (
            self_packs[0].astype(WIDE) + self_got.astype(WIDE),
            out_packs[0].astype(WIDE) + out_got.astype(WIDE),
        ),
        axis=1,
    )
    self_total = place.sum_rows(self_total)
    grad_part = sum(dot_nt(self_grads[side], qkv_weights[side]) for side in (1, 0))
    gain_one = gain_part(grad_part, resid, scale_one)
    grad_zero = grad_one + norm_backward(place.team_sum(grad_part), resid, scale_one, gains[0])
    zero_send = lax.dynamic_slice_in_dim(grad_zero, place.far_index * width, width, 1)
    zero_keep = lax.dynamic_slice_in_dim(grad_zero, place.index * width, width, 1)
    zero_got = place.swap_half(zero_send.astype(LOW)).astype(WIDE)
    grad_residual = cotangent + place.in_order(zero_keep, zero_got)

    folded = [
        sum(jnp.roll(diag[:, i], -i, axis=1) for i in range(8)) for diag in diagonals
    ]
    bias_grads = [
        jnp.dot(back_onehot.T, fold.T, precision=lax.Precision.HIGHEST) for fold in folded
    ]
    gain_sums = jnp.stack((gain_one, gain_two, gain_three / team))
    gain_keep, gain_send = place.team_scatter(place.half_columns(gain_sums), 1, WIDE)
    small_send = jnp.concatenate((gain_send.reshape(-1), bias_grads[1].reshape(-1)))
    small_keep = jnp.concatenate((gain_keep.reshape(-1), bias_grads[0].reshape(-1)))
    small = place.sum_all(small_keep + place.swap_half(small_send))
    gain_sums = small[: 3 * width].reshape(3, width)
    part_rows = buckets // (2 * place.rows)
    bias_sum = lax.dynamic_slice_in_dim(
        small[3 * width :].reshape(buckets, heads),
        (place.dp * place.rows + place.row) * part_rows,
        part_rows,
        axis=0,
    )

    def columns_of(array, first, last):
        return array[:, first:last].astype(WIDE)

    return (
        layer_out,
        grad_residual,
        grad_memory,
        gain_sums[0],
        gain_sums[1],
        gain_sums[2],
        columns_of(self_total, 0, inner),
        columns_of(self_total, inner, 2 * inner),
        columns_of(self_total, 2 * inner, 3 * inner),
        columns_of(self_total, 3 * inner, 4 * inner).T,
        columns_of(cross_total, 0, inner),
        columns_of(cross_total, inner, 2 * inner),
        columns_of(cross_total, 2 * inner, 3 * inner),
        columns_of(cross_total, 3 * inner, 4 * inner).T,
        columns_of(ffn_grads, 0, units),
        columns_of(ffn_grads, units, 2 * units).T,
        bias_sum,
    )


def solution(mesh):
    in_specs = (
        P(None, ("dp", "row"), "col"),
        P(None, ("dp", "row"), "col"),
        P(None, ("dp", "row")),
        P(),
        P(None, ("dp", "row"), "col"),
        P("col"),
        P("col"),
        P("col"),
        P("row", "col"),
        P("row", "col"),
        P("row", "col"),
        P("col", "row"),
        P("row", "col"),
        P("row", "col"),
        P("row", "col"),
        P("col", "row"),
        P("row", "col"),
        P("col", "row"),
        P("row", "col"),
    )
    out_specs = (
        P(None, ("dp", "row"), "col"),
        P(None, ("dp", "row"), "col"),
        P(None, ("dp", "row"), "col"),
        P("col"),
        P("col"),
        P("col"),
        P(("dp", "row"), "col"),
        P(("dp", "row"), "col"),
        P(("dp", "row"), "col"),
        P("col", ("dp", "row")),
        P(("dp", "row"), "col"),
        P(("dp", "row"), "col"),
        P(("dp", "row"), "col"),
        P("col", ("dp", "row")),
        P(("dp", "row"), "col"),
        P("col", ("dp", "row")),
        P(("dp", "row"), "col"),
    )
    return jax.shard_map(body, mesh=mesh, in_specs=in_specs, out_specs=out_specs, check_vma=False)
```
